32 devices in a mesh: groups: 2 (over x), ctx: 16 (over z, y, core).
Axes of the slice: x: 2, y: 2, z: 4, core: 2. Of those that a mesh axis runs over, the one named last changes fastest.
Arguments:
- queries: bfloat16 [6144, 4096], P(('groups', 'ctx')), parts along dimension 0, may hold values from -2.390625 to 2.390625
- keys: bfloat16 [6144, 4096], P(('groups', 'ctx')), parts along dimension 0, may hold values from -2.390625 to 2.390625
- values: bfloat16 [6144, 4096], P(('groups', 'ctx')), parts along dimension 0, may hold values from -6 to 6
- carried_state: float32 [64, 128, 128], P('groups', 'ctx'), parts along dimension 0, may hold values from -6 to 6
- gain: float32 [4096], replicated, may hold values from 0.5 to 1.5
- out_grad: bfloat16 [6144, 4096], P(('groups', 'ctx')), parts along dimension 0, may hold values from -3 to 3
Outputs:
- attended: bfloat16 [6144, 4096], P(('groups', 'ctx')), parts along dimension 0
- q_grad: bfloat16 [6144, 4096], P(('groups', 'ctx')), parts along dimension 0
- k_grad: bfloat16 [6144, 4096], P(('groups', 'ctx')), parts along dimension 0
- v_grad: bfloat16 [6144, 4096], P(('groups', 'ctx')), parts along dimension 0
- state_grad: float32 [64, 128, 128], P('groups', 'ctx'), parts along dimension 0
The draws below stay inside these ranges and needn't reach their ends.
There are 2 independent parts, one for each index of `groups`. The reference program is written for one: setup_inputs(seed, part) draws one part's arguments, and reference() takes and returns one part's arrays. A program takes and returns all parts, laid end to end along the dimension named above; an argument that names none is the same for every part. Nothing has to cross between parts.
All inputs are finite; a program needn't handle non-finite values.
Results may differ from the reference program's by a relative error of at most 0.0075.
Values may be sent and summed in bfloat16 or wider, within the bound.
No kernel may reach another device: no remote copies, remote signals or barrier semaphores. Data moves between devices by JAX's collectives and lax.ppermute only.
A program may use at most 128 MiB of HBM per device.

```python
import jax
import jax.numpy as jnp
from jax import lax

HEADS = 32
HD = 128
TOK_DEV = 192
WIDTH = 4096
SEQ = 3072


def block_levels(key, shape, cuts, smallest, top_value):
    level, own = 1.0, jax.random.fold_in(key, 6)
    for axis_at, shards_of in cuts:
        draws = jnp.exp(jax.random.uniform(jax.random.fold_in(own, axis_at), (shards_of,), jnp.float32, smallest / len(cuts), top_value / len(cuts)))
        level = level * jnp.repeat(draws, shape[axis_at] // shards_of).reshape([-1 if axis == axis_at else 1 for axis in range(len(shape))])
    return level


def gaussian(key, extent, deviation, reach, pieces=(), held_as=jnp.bfloat16):
    values = jax.random.normal(key, extent, jnp.float32) * deviation
    if len(pieces) > 0:
        values = block_levels(key, extent, pieces, -0.22, 0.18) * values
    return jnp.clip(values, min=-reach, max=reach).astype(held_as)


def setup_inputs(seed: int = 0, part: int = 0) -> dict:
    key_of = jax.random.split(jax.random.key(seed), 7)
    part_keys = jax.random.split(jax.random.fold_in(key_of[6], part), 7)
    queries = gaussian(part_keys[0], (SEQ, WIDTH), 0.3, 2.390625, ((0, 16),))
    keys = gaussian(part_keys[1], (SEQ, WIDTH), 0.3, 2.390625, ((0, 16),))
    values = gaussian(part_keys[2], (SEQ, WIDTH), 1.0, 6.0, ((0, 16),))
    carried_state = gaussian(part_keys[3], (HEADS, HD, HD), 1.0, 6.0, ((1, 16),), jnp.float32)
    gain = jnp.clip(1.0 + 0.1 * jax.random.normal(key_of[4], (WIDTH,), jnp.float32), 0.5, 1.5)
    out_grad = gaussian(part_keys[5], (SEQ, WIDTH), 0.5, 3.0, ((0, 16),))
    return dict(queries=queries, keys=keys, values=values, carried_state=carried_state, gain=gain, out_grad=out_grad)


def reference(queries, keys, values, carried_state, gain, out_grad):
    blocks = SEQ // TOK_DEV

    def split(array):
        return array.reshape(blocks, TOK_DEV, HEADS, HD)
    row_ids = lax.broadcasted_iota(jnp.int32, (TOK_DEV, TOK_DEV), 0)
    col_ids = lax.broadcasted_iota(jnp.int32, (TOK_DEV, TOK_DEV), 1)
    causal = (col_ids <= row_ids)[None]
    gain_heads = gain.reshape(1, HEADS, HD)

    def forward(state, inputs):
        query_blk, key_blk, value_blk, dout_blk = inputs
        qf = query_blk.astype(jnp.float32)
        kf = key_blk.astype(jnp.float32)
        vf = value_blk.astype(jnp.float32)
        prior_bf = state.astype(jnp.bfloat16)
        scores = jnp.einsum('thd,shd->hts', qf, kf)
        scores_bf = jnp.where(causal, scores, 0.0).astype(jnp.bfloat16)
        mixed = jnp.einsum('hts,she->the', scores_bf.astype(jnp.float32), vf) + jnp.einsum('thd,hde->the', qf, prior_bf.astype(jnp.float32))
        inv_rms = lax.rsqrt(lax.optimization_barrier(jnp.mean(mixed * mixed, axis=2, keepdims=True)) + 1e-06)
        attended = (gain_heads * mixed * inv_rms).astype(jnp.bfloat16)
        scaled = gain_heads * dout_blk.astype(jnp.float32)
        grad_mixed = (inv_rms * scaled - mixed * (inv_rms * inv_rms * inv_rms) * lax.optimization_barrier(jnp.mean(scaled * mixed, axis=2, keepdims=True))).astype(jnp.bfloat16)
        new_state = state + jnp.einsum('thd,the->hde', kf, vf)
        return (new_state, (attended, grad_mixed, prior_bf, scores_bf))
    xs = (split(queries), split(keys), split(values), split(out_grad))
    _, (attended, grad_mixed, priors, scores_all) = lax.scan(forward, carried_state.astype(jnp.float32), xs)

    def backward(later_state, inputs):
        query_blk, key_blk, value_blk, grad_blk, prior_bf, scores_bf = inputs
        qf = query_blk.astype(jnp.float32)
        kf = key_blk.astype(jnp.float32)
        vf = value_blk.astype(jnp.float32)
        gf = grad_blk.astype(jnp.float32)
        later_bf = later_state.astype(jnp.bfloat16).astype(jnp.float32)
        grad_scores = jnp.einsum('the,she->hts', gf, vf)
        grad_scores = jnp.where(causal, grad_scores, 0.0).astype(jnp.bfloat16).astype(jnp.float32)
        q_grad = jnp.einsum('hts,shd->thd', grad_scores, kf) + jnp.einsum('the,hde->thd', gf, prior_bf.astype(jnp.float32))
        k_grad = jnp.einsum('hts,thd->shd', grad_scores, qf) + jnp.einsum('she,hde->shd', vf, later_bf)
        v_grad = jnp.einsum('hts,the->she', scores_bf.astype(jnp.float32), gf) + jnp.einsum('shd,hde->she', kf, later_bf)
        new_state = later_state + jnp.einsum('thd,the->hde', qf, gf)
        return (new_state, (q_grad.astype(jnp.bfloat16), k_grad.astype(jnp.bfloat16), v_grad.astype(jnp.bfloat16)))
    ys = (xs[0], xs[1], xs[2], grad_mixed, priors, scores_all)
    state_grad, (q_grad, k_grad, v_grad) = lax.scan(backward, jnp.zeros((HEADS, HD, HD), jnp.float32), ys, reverse=True)

    def merge(array):
        return array.reshape(SEQ, WIDTH)
    return (merge(attended), merge(q_grad), merge(k_grad), merge(v_grad), state_grad)
```

```python
import functools

import jax
import jax.numpy as jnp
from jax import lax
from jax.experimental import pallas as pl
from jax.experimental.pallas import tpu as pltpu
from jax.sharding import PartitionSpec as P

BF16 = jnp.bfloat16
F32 = jnp.float32
CHUNKS = 1
HEAD_BLOCK = 4


def causal_mask(count):
    row_ids = lax.broadcasted_iota(jnp.int32, (count, count), 0)
    col_ids = lax.broadcasted_iota(jnp.int32, (count, count), 1)
    return col_ids <= row_ids


def plain_on_device(queries, keys, values, carried_state, gain, out_grad):
    tokens = queries.shape[0]
    heads = carried_state.shape[0]
    head_dim = carried_state.shape[2]
    f32 = dict(preferred_element_type=F32)
    split = lambda a: a.reshape(tokens, heads, head_dim)
    spread = functools.partial(
        lax.all_to_all, axis_name="ctx", split_axis=2, concat_axis=0, tiled=True
    )
    collect = functools.partial(
        lax.all_to_all, axis_name="ctx", split_axis=0, concat_axis=2, tiled=True
    )
    q, k, v = split(queries), split(keys), split(values)
    blocks = spread(jnp.einsum("thd,the->hde", k, v, **f32)[None])
    earlier = jnp.cumsum(blocks, axis=0) - blocks + carried_state[None]
    prior_bf = collect(earlier)[0].astype(BF16)
    causal = causal_mask(tokens)[None]
    scores = jnp.where(causal, jnp.einsum("thd,shd->hts", q, k, **f32), 0.0).astype(BF16)
    mixed = jnp.einsum("hts,she->the", scores, v, **f32)
    mixed = mixed + jnp.einsum("thd,hde->the", q, prior_bf, **f32)
    inv_rms = lax.rsqrt(jnp.mean(mixed * mixed, axis=2, keepdims=True) + 1e-06)
    gain_heads = gain.reshape(1, heads, head_dim)
    attended = (gain_heads * mixed * inv_rms).astype(BF16)
    scaled = gain_heads * split(out_grad).astype(F32)
    grad_mixed = (
        inv_rms * scaled
        - mixed * (inv_rms * inv_rms * inv_rms) * jnp.mean(scaled * mixed, axis=2, keepdims=True)
    ).astype(BF16)
    grads = spread(jnp.einsum("thd,the->hde", q, grad_mixed, **f32)[None])
    inclusive = jnp.cumsum(grads, axis=0)
    total = inclusive[-1:]
    later_bf = collect((total - inclusive).astype(BF16))[0]
    grad_scores = jnp.einsum("the,she->hts", grad_mixed, v, **f32)
    grad_scores = jnp.where(causal, grad_scores, 0.0).astype(BF16)
    q_grad = jnp.einsum("hts,shd->thd", grad_scores, k, **f32)
    q_grad = q_grad + jnp.einsum("the,hde->thd", grad_mixed, prior_bf, **f32)
    k_grad = jnp.einsum("hts,thd->shd", grad_scores, q, **f32)
    k_grad = k_grad + jnp.einsum("she,hde->shd", v, later_bf, **f32)
    v_grad = jnp.einsum("hts,the->she", scores, grad_mixed, **f32)
    v_grad = v_grad + jnp.einsum("shd,hde->she", k, later_bf, **f32)
    flat = lambda a: a.astype(BF16).reshape(tokens, heads * head_dim)
    return flat(attended), flat(q_grad), flat(k_grad), flat(v_grad), total[0]


def dot(a, b, dims):
    return lax.dot_general(a, b, (dims, ((), ())), preferred_element_type=F32)


NN = ((1,), (0,))
NT = ((1,), (1,))
TN = ((0,), (0,))


def put_halves(core, state, h, mine_ref, theirs_ref):
    slabs = mine_ref.shape[2] // 8
    for slab in range(slabs):
        for pair in range(2):
            at = 8 * (4 * slab + 2 * pair)
            even, odd = state[at : at + 8], state[at + 8 : at + 16]
            rows = slice(8 * slab, 8 * slab + 8)
            mine_ref[pair, h, rows, :] = jnp.where(core == 0, even, odd)
            theirs_ref[pair, h, rows, :] = jnp.where(core == 0, odd, even).astype(BF16)


def whole_state(core, own_ref, got_ref, h):
    slabs = own_ref.shape[2] // 8
    own = [own_ref[pair, h].astype(F32) for pair in range(2)]
    got = [got_ref[pair, h].astype(F32) for pair in range(2)]
    even = [jnp.where(core == 0, own[pair], got[pair]) for pair in range(2)]
    odd = [jnp.where(core == 0, got[pair], own[pair]) for pair in range(2)]
    tiles = []
    for slab in range(slabs):
        for pair in range(2):
            rows = slice(8 * slab, 8 * slab + 8)
            tiles += [even[pair][rows], odd[pair][rows]]
    return jnp.concatenate(tiles, axis=0).astype(BF16)


def cols(h, dim):
    return slice(h * dim, (h + 1) * dim)


def state_kernel(core_ref, k_ref, v_ref, mine_ref, theirs_ref):
    core = core_ref[0]
    dim = mine_ref.shape[3]
    for h in range(mine_ref.shape[1]):
        state = dot(k_ref[:, cols(h, dim)], v_ref[:, cols(h, dim)], TN)
        put_halves(core, state, h, mine_ref, theirs_ref)


def intra_kernel(q_ref, k_ref, v_ref, scores_ref, intra_ref):
    tokens = q_ref.shape[0]
    heads = scores_ref.shape[0]
    dim = q_ref.shape[1] // heads
    causal = causal_mask(tokens)
    for h in range(heads):
        at = cols(h, dim)
        scores = jnp.where(causal, dot(q_ref[:, at], k_ref[:, at], NT), 0.0).astype(BF16)
        scores_ref[h] = scores
        intra_ref[:, at] = dot(scores, v_ref[:, at], NN)


def mix_kernel(core_ref, q_ref, intra_ref, own_ref, got_ref, gain_ref, do_ref, *rest):
    att_ref, gm_ref, prior_ref, mine_ref, theirs_ref = rest[-5:]
    core = core_ref[0]
    heads, dim = own_ref.shape[1], own_ref.shape[3]
    for h in range(heads):
        at = cols(h, dim)
        prior = whole_state(core, own_ref, got_ref, h)
        prior_ref[h] = prior
        q = q_ref[:, at]
        mixed = intra_ref[:, at] + dot(q, prior, NN)
        gain = gain_ref[:, at]
        inv = lax.rsqrt(jnp.mean(mixed * mixed, axis=1, keepdims=True) + 1e-06)
        att_ref[:, at] = (gain * mixed * inv).astype(BF16)
        scaled = gain * do_ref[:, at].astype(F32)
        along = jnp.mean(scaled * mixed, axis=1, keepdims=True)
        gm = (inv * scaled - mixed * (inv * inv * inv * along)).astype(BF16)
        gm_ref[:, at] = gm
        put_halves(core, dot(q, gm, TN), h, mine_ref, theirs_ref)


def local_grad_kernel(q_ref, k_ref, v_ref, gm_ref, scores_ref, prior_ref, *rest):
    qg_ref, kpart_ref, vpart_ref = rest[-3:]
    tokens = q_ref.shape[0]
    heads = scores_ref.shape[0]
    dim = q_ref.shape[1] // heads
    causal = causal_mask(tokens)
    for h in range(heads):
        at = cols(h, dim)
        gm = gm_ref[:, at]
        gs = jnp.where(causal, dot(gm, v_ref[:, at], NT), 0.0).astype(BF16)
        qg = dot(gs, k_ref[:, at], NN) + dot(gm, prior_ref[h], NT)
        qg_ref[:, at] = qg.astype(BF16)
        kpart_ref[:, at] = dot(gs, q_ref[:, at], TN)
        vpart_ref[:, at] = dot(scores_ref[h], gm, TN)


def final_kernel(core_ref, k_ref, v_ref, kpart_ref, vpart_ref, own_ref, got_ref, *rest):
    kg_ref, vg_ref = rest[-2:]
    core = core_ref[0]
    heads, dim = own_ref.shape[1], own_ref.shape[3]
    for h in range(heads):
        at = cols(h, dim)
        later = whole_state(core, own_ref, got_ref, h)
        kg_ref[:, at] = (kpart_ref[:, at] + dot(v_ref[:, at], later, NT)).astype(BF16)
        vg_ref[:, at] = (vpart_ref[:, at] + dot(k_ref[:, at], later, NN)).astype(BF16)


def fused_on_device(n, queries, keys, values, carried_state, gain, out_grad):
    tokens, width = queries.shape
    heads, owned, dim = carried_state.shape
    slab_rows = dim // 4
    part = heads // CHUNKS
    hb = HEAD_BLOCK
    steps = part // hb
    rank = lax.axis_index("ctx")
    core, pair, slab = rank % 2, (rank // 2) % 2, rank // 4
    core_arg = core.reshape(1).astype(jnp.int32)
    gain_row = gain.reshape(1, width)

    def swap(x, bit):
        return lax.ppermute(x, "ctx", [(i, i ^ bit) for i in range(n)])

    def call(body, chunk, ins, outs, flops, with_core=True, keep=()):
        off = chunk * steps
        specs = {
            "flat": lambda o: pl.BlockSpec((tokens, hb * dim), lambda i, *_: (0, i + o)),
            "row": lambda o: pl.BlockSpec((1, hb * dim), lambda i, *_: (0, i + o)),
            "half": lambda o: pl.BlockSpec((2, hb, slab_rows, dim), lambda i, *_: (0, i, 0, 0)),
            "sq": lambda o: pl.BlockSpec((hb, tokens, tokens), lambda i, *_: (i, 0, 0)),
            "state": lambda o: pl.BlockSpec((hb, dim, dim), lambda i, *_: (i, 0, 0)),
            "local": lambda o: pl.BlockSpec((tokens, hb * dim), lambda i, *_: (0, i)),
        }
        shapes = {
            "flat": (tokens, width),
            "half": (2, part, slab_rows, dim),
            "sq": (part, tokens, tokens),
            "state": (part, dim, dim),
            "local": (tokens, part * dim),
        }
        scalars = 1 if with_core else 0
        args = [a for _, a in ins]
        in_specs = [specs[kind](off) for kind, _ in ins]
        aliases = {}
        for at, array in keep:
            aliases[scalars + len(args)] = at
            args.append(array)
            in_specs.append(pl.BlockSpec(memory_space=pl.ANY))
        out_shape = [jax.ShapeDtypeStruct(shapes[kind], t) for kind, t in outs]
        moved = sum(a.size * a.dtype.itemsize for _, a in ins) // CHUNKS
        moved += sum(s.size * s.dtype.itemsize for s in out_shape)
        return pl.pallas_call(
            body,
            out_shape=out_shape,
            grid_spec=pltpu.PrefetchScalarGridSpec(
                num_scalar_prefetch=scalars,
                grid=(steps,),
                in_specs=in_specs,
                out_specs=[specs[kind](off) for kind, _ in outs],
            ),
            input_output_aliases=aliases,
            cost_estimate=pl.CostEstimate(
                flops=int(flops * part), bytes_accessed=int(moved), transcendentals=0
            ),
            compiler_params=pltpu.CompilerParams(vmem_limit_bytes=32 * 1024 * 1024),
        )(*([core_arg] if with_core else []), *args)

    def scan_out(mine, theirs, start, later):
        bit = lambda x: (x == 0) if later else (x == 1)
        from_core = swap(theirs, 1).astype(F32)
        chip = mine + from_core
        kept = jnp.where(pair == 0, chip[0], chip[1])
        from_pair = swap(jnp.where(pair == 0, chip[1], chip[0]).astype(BF16), 2).astype(F32)
        total = kept + from_pair
        before = start
        step = 1
        while 4 * step < n:
            got = swap(total.astype(BF16), 4 * step).astype(F32)
            before = before + jnp.where(bit((slab // step) % 2), got, 0.0)
            total = total + got
            step *= 2
        for_pair = before + jnp.where(bit(1 - pair), kept, 0.0)
        here = before + jnp.where(bit(pair), from_pair, 0.0)
        there = swap(for_pair.astype(BF16), 2).astype(F32)
        ours = jnp.stack([jnp.where(pair == 0, here, there), jnp.where(pair == 0, there, here)])
        got_half = swap((ours + jnp.where(bit(1 - core), mine, 0.0)).astype(BF16), 1)
        own_half = ours + jnp.where(bit(core), from_core, 0.0)
        return own_half.astype(BF16), got_half, total

    carried = carried_state.astype(BF16)[:, None]
    step = 1
    while 4 * step < n:
        other = swap(carried, 4 * step)
        upper = (slab // step) % 2 == 1
        carried = jnp.concatenate(
            [jnp.where(upper, other, carried), jnp.where(upper, carried, other)], axis=1
        )
        step *= 2
    carried = carried.reshape(heads, slab_rows, dim).astype(F32)

    mac = 2 * tokens * dim
    states, intras, priors, mixes, locals_ = [], [], [], [], []
    for g in range(CHUNKS):
        ins = [("flat", keys), ("flat", values)]
        states.append(call(state_kernel, g, ins, [("half", F32), ("half", BF16)], mac * dim))
    for g in range(CHUNKS):
        ins = [("flat", queries), ("flat", keys), ("flat", values)]
        outs = [("sq", BF16), ("local", F32)]
        intras.append(call(intra_kernel, g, ins, outs, 2 * mac * tokens, with_core=False))
    for g in range(CHUNKS):
        start = carried[g * part : (g + 1) * part]
        priors.append(scan_out(*states[g], start, False))
    attended = None
    for g in range(CHUNKS):
        ins = [
            ("flat", queries),
            ("local", intras[g][1]),
            ("half", priors[g][0]),
            ("half", priors[g][1]),
            ("row", gain_row),
            ("flat", out_grad),
        ]
        outs = [("flat", BF16), ("local", BF16), ("state", BF16), ("half", F32), ("half", BF16)]
        keep = [] if attended is None else [(0, attended)]
        mixes.append(call(mix_kernel, g, ins, outs, 2 * mac * dim, keep=keep))
        attended = mixes[g][0]
    q_grad = None
    for g in range(CHUNKS):
        ins = [
            ("flat", queries),
            ("flat", keys),
            ("flat", values),
            ("local", mixes[g][1]),
            ("sq", intras[g][0]),
            ("state", mixes[g][2]),
        ]
        outs = [("flat", BF16), ("local", F32), ("local", F32)]
        keep = [] if q_grad is None else [(0, q_grad)]
        flops = 4 * mac * tokens + mac * dim
        locals_.append(call(local_grad_kernel, g, ins, outs, flops, with_core=False, keep=keep))
        q_grad = locals_[g][0]
    laters = [scan_out(mixes[g][3], mixes[g][4], jnp.zeros((), F32), True) for g in range(CHUNKS)]
    finals = None
    for g in range(CHUNKS):
        ins = [
            ("flat", keys),
            ("flat", values),
            ("local", locals_[g][1]),
            ("local", locals_[g][2]),
            ("half", laters[g][0]),
            ("half", laters[g][1]),
        ]
        keep = [] if finals is None else [(0, finals[0]), (1, finals[1])]
        finals = call(final_kernel, g, ins, [("flat", BF16)] * 2, 2 * mac * dim, keep=keep)
    total = jnp.concatenate([later[2] for later in laters], axis=0)
    state_grad = lax.dynamic_slice_in_dim(total, slab * owned, owned, axis=1)
    return attended, q_grad, finals[0], finals[1], state_grad


def on_device(n, queries, keys, values, carried_state, gain, out_grad):
    heads, owned, dim = carried_state.shape
    power = n >= 4 and (n & (n - 1)) == 0
    fits = power and owned % 8 == 0 and owned == 8 and dim % 128 == 0
    if fits and heads % (CHUNKS * HEAD_BLOCK) == 0 and queries.shape[0] % 16 == 0:
        return fused_on_device(n, queries, keys, values, carried_state, gain, out_grad)
    return plain_on_device(queries, keys, values, carried_state, gain, out_grad)


def solution(mesh):
    rows = P(("groups", "ctx"), None)
    state = P("groups", "ctx", None)
    return jax.shard_map(
        functools.partial(on_device, mesh.shape["ctx"]),
        mesh=mesh,
        in_specs=(rows, rows, rows, state, P(), rows),
        out_specs=(rows, rows, rows, rows, state),
        check_vma=False,
    )
```

```python
import functools
import math

import jax
import jax.numpy as jnp
from jax import lax
from jax.experimental import pallas as pl
from jax.experimental.pallas import tpu as pltpu
from jax.sharding import PartitionSpec as P


BF16 = jnp.bfloat16
F32 = jnp.float32
CHUNKS = 2
HEAD_BLOCK = 4
LOCAL_SPLIT = 2
VMEM_LIMIT = 6 * 1024 * 1024


def causal_mask(count):
    row_ids = lax.broadcasted_iota(jnp.int32, (count, count), 0)
    col_ids = lax.broadcasted_iota(jnp.int32, (count, count), 1)
    return col_ids <= row_ids


def plain_on_device(queries, keys, values, carried_state, gain, out_grad):
    tokens = queries.shape[0]
    heads = carried_state.shape[0]
    head_dim = carried_state.shape[2]
    f32 = dict(preferred_element_type=F32)
    split = lambda a: a.reshape(tokens, heads, head_dim)
    spread = functools.partial(
        lax.all_to_all, axis_name="ctx", split_axis=2, concat_axis=0, tiled=True
    )
    collect = functools.partial(
        lax.all_to_all, axis_name="ctx", split_axis=0, concat_axis=2, tiled=True
    )
    q, k, v = split(queries), split(keys), split(values)
    blocks = spread(jnp.einsum("thd,the->hde", k, v, **f32)[None])
    earlier = jnp.cumsum(blocks, axis=0) - blocks + carried_state[None]
    prior_bf = collect(earlier)[0].astype(BF16)
    causal = causal_mask(tokens)[None]
    scores = jnp.where(causal, jnp.einsum("thd,shd->hts", q, k, **f32), 0.0).astype(BF16)
    mixed = jnp.einsum("hts,she->the", scores, v, **f32)
    mixed = mixed + jnp.einsum("thd,hde->the", q, prior_bf, **f32)
    inv_rms = lax.rsqrt(jnp.mean(mixed * mixed, axis=2, keepdims=True) + 1e-06)
    gain_heads = gain.reshape(1, heads, head_dim)
    attended = (gain_heads * mixed * inv_rms).astype(BF16)
    scaled = gain_heads * split(out_grad).astype(F32)
    grad_mixed = (
        inv_rms * scaled
        - mixed * (inv_rms * inv_rms * inv_rms) * jnp.mean(scaled * mixed, axis=2, keepdims=True)
    ).astype(BF16)
    grads = spread(jnp.einsum("thd,the->hde", q, grad_mixed, **f32)[None])
    inclusive = jnp.cumsum(grads, axis=0)
    total = inclusive[-1:]
    later_bf = collect((total - inclusive).astype(BF16))[0]
    grad_scores = jnp.einsum("the,she->hts", grad_mixed, v, **f32)
    grad_scores = jnp.where(causal, grad_scores, 0.0).astype(BF16)
    q_grad = jnp.einsum("hts,shd->thd", grad_scores, k, **f32)
    q_grad = q_grad + jnp.einsum("the,hde->thd", grad_mixed, prior_bf, **f32)
    k_grad = jnp.einsum("hts,thd->shd", grad_scores, q, **f32)
    k_grad = k_grad + jnp.einsum("she,hde->shd", v, later_bf, **f32)
    v_grad = jnp.einsum("hts,the->she", scores, grad_mixed, **f32)
    v_grad = v_grad + jnp.einsum("shd,hde->she", k, later_bf, **f32)
    flat = lambda a: a.astype(BF16).reshape(tokens, heads * head_dim)
    return flat(attended), flat(q_grad), flat(k_grad), flat(v_grad), total[0]


def dot(a, b, dims):
    return lax.dot_general(a, b, (dims, ((), ())), preferred_element_type=F32)


NN = ((1,), (0,))
NT = ((1,), (1,))
TN = ((0,), (0,))


def put_halves(core, state, h, mine_ref, theirs_ref):
    slabs = mine_ref.shape[2] // 8
    for slab in range(slabs):
        for pair in range(2):
            at = 8 * (4 * slab + 2 * pair)
            even, odd = state[at : at + 8], state[at + 8 : at + 16]
            rows = slice(8 * slab, 8 * slab + 8)
            mine_ref[pair, h, rows, :] = jnp.where(core == 0, even, odd)
            theirs_ref[pair, h, rows, :] = jnp.where(core == 0, odd, even).astype(BF16)


def whole_state(core, own_ref, got_ref, h):
    slabs = own_ref.shape[2] // 8
    own = [own_ref[pair, h].astype(F32) for pair in range(2)]
    got = [got_ref[pair, h].astype(F32) for pair in range(2)]
    even = [jnp.where(core == 0, own[pair], got[pair]) for pair in range(2)]
    odd = [jnp.where(core == 0, got[pair], own[pair]) for pair in range(2)]
    tiles = []
    for slab in range(slabs):
        for pair in range(2):
            rows = slice(8 * slab, 8 * slab + 8)
            tiles += [even[pair][rows], odd[pair][rows]]
    return jnp.concatenate(tiles, axis=0).astype(BF16)


def cols(h, dim):
    return slice(h * dim, (h + 1) * dim)


def state_kernel(core_ref, k_ref, v_ref, mine_ref, theirs_ref):
    core = core_ref[0]
    dim = mine_ref.shape[3]
    ats = [cols(h, dim) for h in range(mine_ref.shape[1])]
    states = [dot(k_ref[:, at], v_ref[:, at], TN) for at in ats]
    for h, state in enumerate(states):
        put_halves(core, state, h, mine_ref, theirs_ref)


def intra_kernel(q_ref, k_ref, v_ref, scores_ref, intra_ref):
    heads = scores_ref.shape[0]
    dim = q_ref.shape[1] // heads
    causal = causal_mask(q_ref.shape[0])
    ats = [cols(h, dim) for h in range(heads)]
    scores = [
        jnp.where(causal, dot(q_ref[:, at], k_ref[:, at], NT), 0.0).astype(BF16) for at in ats
    ]
    for h, at in enumerate(ats):
        scores_ref[h] = scores[h]
        intra_ref[:, at] = dot(scores[h], v_ref[:, at], NN)


def mix_kernel(core_ref, q_ref, intra_ref, own_ref, got_ref, gain_ref, do_ref, *rest):
    att_ref, gm_ref, prior_ref, mine_ref, theirs_ref = rest[-5:]
    core = core_ref[0]
    heads, dim = own_ref.shape[1], own_ref.shape[3]
    ats = [cols(h, dim) for h in range(heads)]
    for h in range(heads):
        prior_ref[h] = whole_state(core, own_ref, got_ref, h)
    crosses = [dot(q_ref[:, at], prior_ref[h], NN) for h, at in enumerate(ats)]
    for at, cross in zip(ats, crosses):
        mixed = intra_ref[:, at] + cross
        gain = gain_ref[:, at]
        inv = lax.rsqrt(jnp.mean(mixed * mixed, axis=1, keepdims=True) + 1e-06)
        att_ref[:, at] = (gain * mixed * inv).astype(BF16)
        scaled = gain * do_ref[:, at].astype(F32)
        along = jnp.mean(scaled * mixed, axis=1, keepdims=True)
        gm_ref[:, at] = (inv * scaled - mixed * (inv * inv * inv * along)).astype(BF16)
    grads = [dot(q_ref[:, at], gm_ref[:, at], TN) for at in ats]
    for h, grad in enumerate(grads):
        put_halves(core, grad, h, mine_ref, theirs_ref)


def local_grad_kernel(q_ref, k_ref, v_ref, gm_ref, scores_ref, prior_ref, *rest):
    qg_ref, kpart_ref, vpart_ref = rest[-3:]
    heads = scores_ref.shape[0]
    dim = q_ref.shape[1] // heads
    causal = causal_mask(q_ref.shape[0])
    ats = [cols(h, dim) for h in range(heads)]
    grads = [
        jnp.where(causal, dot(gm_ref[:, at], v_ref[:, at], NT), 0.0).astype(BF16) for at in ats
    ]
    for h, at in enumerate(ats):
        qg = dot(grads[h], k_ref[:, at], NN) + dot(gm_ref[:, at], prior_ref[h], NT)
        qg_ref[:, at] = qg.astype(BF16)
    for h, at in enumerate(ats):
        kpart_ref[:, at] = dot(grads[h], q_ref[:, at], TN)
    for h, at in enumerate(ats):
        vpart_ref[:, at] = dot(scores_ref[h], gm_ref[:, at], TN)


def final_kernel(core_ref, k_ref, v_ref, kpart_ref, vpart_ref, own_ref, got_ref, *rest):
    kg_ref, vg_ref = rest[-2:]
    core = core_ref[0]
    heads, dim = own_ref.shape[1], own_ref.shape[3]
    laters = [whole_state(core, own_ref, got_ref, h) for h in range(heads)]
    for h, later in enumerate(laters):
        at = cols(h, dim)
        kg_ref[:, at] = (kpart_ref[:, at] + dot(v_ref[:, at], later, NT)).astype(BF16)
    for h, later in enumerate(laters):
        at = cols(h, dim)
        vg_ref[:, at] = (vpart_ref[:, at] + dot(k_ref[:, at], later, NN)).astype(BF16)


def fused_on_device(n, queries, keys, values, carried_state, gain, out_grad):
    tokens, width = queries.shape
    heads, owned, dim = carried_state.shape
    slab_rows = dim // 4
    part = heads // CHUNKS
    hb = HEAD_BLOCK
    rank = lax.axis_index("ctx").astype(jnp.int32)
    core_arg = (rank & 1).reshape(1)
    odd_core, odd_pair = (rank & 1) == 1, (rank & 2) == 2
    odd_slab = {}
    step = 1
    while 4 * step < n:
        odd_slab[step] = (rank & (4 * step)) != 0
        step *= 2
    owned_at = (lax.axis_index("ctx").astype(jnp.uint32) >> 2) * jnp.uint32(owned)
    scalars = (core_arg, odd_core, odd_pair, odd_slab, owned_at)
    scalars, (keys, values, carried_state) = lax.optimization_barrier(
        (scalars, (keys, values, carried_state))
    )
    core_arg, odd_core, odd_pair, odd_slab, owned_at = scalars
    gain_row = gain.reshape(1, width)

    def swap(x, bit):
        return lax.ppermute(x, "ctx", [(i, i ^ bit) for i in range(n)])

    def call(body, chunk, ins, outs, flops, with_core=True, keep=(), sub=0, subs=1):
        count = part // hb // subs
        first = sub * count
        off = chunk * (part // hb) + first
        specs = {
            "flat": pl.BlockSpec((tokens, hb * dim), lambda i, *_: (0, i + off)),
            "row": pl.BlockSpec((1, hb * dim), lambda i, *_: (0, i + off)),
            "half": pl.BlockSpec((2, hb, slab_rows, dim), lambda i, *_: (0, i + first, 0, 0)),
            "sq": pl.BlockSpec((hb, tokens, tokens), lambda i, *_: (i + first, 0, 0)),
            "state": pl.BlockSpec((hb, dim, dim), lambda i, *_: (i + first, 0, 0)),
            "local": pl.BlockSpec((tokens, hb * dim), lambda i, *_: (0, i + first)),
        }
        shapes = {
            "flat": (tokens, width),
            "half": (2, part, slab_rows, dim),
            "sq": (part, tokens, tokens),
            "state": (part, dim, dim),
            "local": (tokens, part * dim),
        }
        scalar_args = [core_arg] if with_core else []
        args = [a for _, a in ins]
        in_specs = [specs[kind] for kind, _ in ins]
        aliases = {}
        for at, array in keep:
            aliases[len(scalar_args) + len(args)] = at
            args.append(array)
            in_specs.append(pl.BlockSpec(memory_space=pl.ANY))
        block = lambda kind: math.prod(specs[kind].block_shape)
        moved = sum(block(kind) * a.dtype.itemsize for kind, a in ins)
        moved += sum(block(kind) * jnp.dtype(t).itemsize for kind, t in outs)
        return pl.pallas_call(
            body,
            out_shape=[jax.ShapeDtypeStruct(shapes[kind], t) for kind, t in outs],
            grid_spec=pltpu.PrefetchScalarGridSpec(
                num_scalar_prefetch=len(scalar_args),
                grid=(count,),
                in_specs=in_specs,
                out_specs=[specs[kind] for kind, _ in outs],
            ),
            input_output_aliases=aliases,
            cost_estimate=pl.CostEstimate(
                flops=flops * count * hb, bytes_accessed=moved * count, transcendentals=0
            ),
            compiler_params=pltpu.CompilerParams(vmem_limit_bytes=VMEM_LIMIT),
        )(*scalar_args, *args)

    def scan_out(mine, theirs, carried=None):
        later = carried is None

        def if_after(odd, x):
            return jnp.where(odd, 0.0, x) if later else jnp.where(odd, x, 0.0)

        def if_before(odd, x):
            return jnp.where(odd, x, 0.0) if later else jnp.where(odd, 0.0, x)

        from_core = swap(theirs, 1).astype(F32)
        chip = mine + from_core
        kept = jnp.where(odd_pair, chip[1], chip[0])
        sent = jnp.where(odd_pair, chip[0], chip[1]).astype(BF16)
        from_pair = swap(sent, 2).astype(F32)
        total = kept + from_pair
        before = 0.0
        last = max(odd_slab)
        for step, odd in odd_slab.items():
            if later:
                got = swap(total.astype(BF16), 4 * step).astype(F32)
                before = before + if_after(odd, got)
                total = total + got
            elif step < last:
                rows = jnp.concatenate([total.astype(BF16), carried], axis=1)
                rows = swap(rows, 4 * step)
                got, other = rows[:, :slab_rows].astype(F32), rows[:, slab_rows:]
                before = before + if_after(odd, got)
                total = total + got
                lower, upper = jnp.where(odd, other, carried), jnp.where(odd, carried, other)
                carried = jnp.concatenate([lower, upper], axis=1)
            else:
                blank = jnp.zeros_like(carried)
                lower, upper = jnp.where(odd, blank, carried), jnp.where(odd, carried, blank)
                known = jnp.concatenate([lower, upper], axis=1).astype(F32)
                sent = (known + if_before(odd, total)).astype(BF16)
                before = before + known + swap(sent, 4 * step).astype(F32)
        for_pair = (before + if_before(odd_pair, kept)).astype(BF16)
        here = before + if_after(odd_pair, from_pair)
        there = swap(for_pair, 2).astype(F32)
        ours = jnp.stack([jnp.where(odd_pair, there, here), jnp.where(odd_pair, here, there)])
        for_core = (ours + if_before(odd_core, mine)).astype(BF16)
        got_half = swap(for_core, 1)
        own_half = (ours + if_after(odd_core, from_core)).astype(BF16)
        return own_half, got_half, total

    mac = 2 * tokens * dim
    chunks = range(CHUNKS)
    states, intras, priors, mixes, locals_ = [], [], [], [], []
    for g in chunks:
        pair = (keys, values)
        if g == 0:
            pair = [pltpu.with_memory_space_constraint(x, pltpu.HBM) for x in pair]
        ins = [("flat", x) for x in pair]
        outs = [("half", F32), ("half", BF16)]
        states.append(call(state_kernel, g, ins, outs, mac * dim))
    for g in chunks:
        ins = [("flat", queries), ("flat", keys), ("flat", values)]
        outs = [("sq", BF16), ("local", F32)]
        intras.append(call(intra_kernel, g, ins, outs, 2 * mac * tokens, with_core=False))
    for g in chunks:
        carried = carried_state[g * part : (g + 1) * part].astype(BF16)
        priors.append(scan_out(*states[g], carried))
    keep = []
    for g in chunks:
        ins = [
            ("flat", queries),
            ("local", intras[g][1]),
            ("half", priors[g][0]),
            ("half", priors[g][1]),
            ("row", gain_row),
            ("flat", out_grad),
        ]
        outs = [("flat", BF16), ("local", BF16), ("state", BF16), ("half", F32), ("half", BF16)]
        mixes.append(call(mix_kernel, g, ins, outs, 2 * mac * dim, keep=keep))
        keep = [(0, mixes[g][0])]
    keep = []
    for g in chunks:
        ins = [
            ("flat", queries),
            ("flat", keys),
            ("flat", values),
            ("local", mixes[g][1]),
            ("sq", intras[g][0]),
            ("state", mixes[g][2]),
        ]
        outs = [("flat", BF16), ("local", F32), ("local", F32)]
        flops = 4 * mac * tokens + mac * dim
        for sub in range(LOCAL_SPLIT):
            at = dict(sub=sub, subs=LOCAL_SPLIT)
            made = call(local_grad_kernel, g, ins, outs, flops, False, keep, **at)
            keep = list(enumerate(made))
        locals_.append(made)
        keep = [(0, made[0])]
    laters = [scan_out(mixes[g][3], mixes[g][4]) for g in chunks]
    keep = []
    for g in chunks:
        ins = [
            ("flat", keys),
            ("flat", values),
            ("local", locals_[g][1]),
            ("local", locals_[g][2]),
            ("half", laters[g][0]),
            ("half", laters[g][1]),
        ]
        made = call(final_kernel, g, ins, [("flat", BF16)] * 2, 2 * mac * dim, keep=keep)
        keep = list(enumerate(made))
    zero = jnp.uint32(0)
    owned_rows = [
        lax.dynamic_slice(later, (zero, owned_at, zero), (part, owned, dim)) for _, _, later in laters
    ]
    state_grad = jnp.concatenate(owned_rows, axis=0)
    return mixes[-1][0], locals_[-1][0], made[0], made[1], state_grad


def on_device(n, queries, keys, values, carried_state, gain, out_grad):
    heads, owned, dim = carried_state.shape
    power = n >= 4 and (n & (n - 1)) == 0
    fits = power and owned % 8 == 0 and owned == 8 and dim % 128 == 0
    if fits and heads % (CHUNKS * HEAD_BLOCK) == 0 and queries.shape[0] % 16 == 0:
        return fused_on_device(n, queries, keys, values, carried_state, gain, out_grad)
    return plain_on_device(queries, keys, values, carried_state, gain, out_grad)


def solution(mesh):
    rows = P(("groups", "ctx"), None)
    state = P("groups", "ctx", None)
    return jax.shard_map(
        functools.partial(on_device, mesh.shape["ctx"]),
        mesh=mesh,
        in_specs=(rows, rows, rows, state, P(), rows),
        out_specs=(rows, rows, rows, rows, state),
        check_vma=False,
    )
```

```python
import functools
import math

import jax
import jax.numpy as jnp
from jax import lax
from jax.experimental import pallas as pl
from jax.experimental.pallas import tpu as pltpu
from jax.sharding import PartitionSpec as P


BF16 = jnp.bfloat16
F32 = jnp.float32
CHUNK_EIGHTHS = (4, 4)
BLOCKS = {"state": 8, "intra": 16, "mix": 16, "local": 16, "final": 16}
LOCAL_SPLIT = 1
VMEM_LIMIT = 20 * 1024 * 1024


def causal_mask(count):
    row_ids = lax.broadcasted_iota(jnp.int32, (count, count), 0)
    col_ids = lax.broadcasted_iota(jnp.int32, (count, count), 1)
    return col_ids <= row_ids


def plain_on_device(queries, keys, values, carried_state, gain, out_grad):
    tokens = queries.shape[0]
    heads = carried_state.shape[0]
    head_dim = carried_state.shape[2]
    f32 = dict(preferred_element_type=F32)
    split = lambda a: a.reshape(tokens, heads, head_dim)
    spread = functools.partial(
        lax.all_to_all, axis_name="ctx", split_axis=2, concat_axis=0, tiled=True
    )
    collect = functools.partial(
        lax.all_to_all, axis_name="ctx", split_axis=0, concat_axis=2, tiled=True
    )
    q, k, v = split(queries), split(keys), split(values)
    blocks = spread(jnp.einsum("thd,the->hde", k, v, **f32)[None])
    earlier = jnp.cumsum(blocks, axis=0) - blocks + carried_state[None]
    prior_bf = collect(earlier)[0].astype(BF16)
    causal = causal_mask(tokens)[None]
    scores = jnp.where(causal, jnp.einsum("thd,shd->hts", q, k, **f32), 0.0).astype(BF16)
    mixed = jnp.einsum("hts,she->the", scores, v, **f32)
    mixed = mixed + jnp.einsum("thd,hde->the", q, prior_bf, **f32)
    inv_rms = lax.rsqrt(jnp.mean(mixed * mixed, axis=2, keepdims=True) + 1e-06)
    gain_heads = gain.reshape(1, heads, head_dim)
    attended = (gain_heads * mixed * inv_rms).astype(BF16)
    scaled = gain_heads * split(out_grad).astype(F32)
    grad_mixed = (
        inv_rms * scaled
        - mixed * (inv_rms * inv_rms * inv_rms) * jnp.mean(scaled * mixed, axis=2, keepdims=True)
    ).astype(BF16)
    grads = spread(jnp.einsum("thd,the->hde", q, grad_mixed, **f32)[None])
    inclusive = jnp.cumsum(grads, axis=0)
    total = inclusive[-1:]
    later_bf = collect((total - inclusive).astype(BF16))[0]
    grad_scores = jnp.einsum("the,she->hts", grad_mixed, v, **f32)
    grad_scores = jnp.where(causal, grad_scores, 0.0).astype(BF16)
    q_grad = jnp.einsum("hts,shd->thd", grad_scores, k, **f32)
    q_grad = q_grad + jnp.einsum("the,hde->thd", grad_mixed, prior_bf, **f32)
    k_grad = jnp.einsum("hts,thd->shd", grad_scores, q, **f32)
    k_grad = k_grad + jnp.einsum("she,hde->shd", v, later_bf, **f32)
    v_grad = jnp.einsum("hts,the->she", scores, grad_mixed, **f32)
    v_grad = v_grad + jnp.einsum("shd,hde->she", k, later_bf, **f32)
    flat = lambda a: a.astype(BF16).reshape(tokens, heads * head_dim)
    return flat(attended), flat(q_grad), flat(k_grad), flat(v_grad), total[0]


def dot(a, b, dims):
    return lax.dot_general(a, b, (dims, ((), ())), preferred_element_type=F32)


NN = ((1,), (0,))
NT = ((1,), (1,))
TN = ((0,), (0,))


def put_halves(core, state, h, mine_ref, theirs_ref):
    slabs = mine_ref.shape[2] // 8
    for slab in range(slabs):
        for pair in range(2):
            at = 8 * (4 * slab + 2 * pair)
            even, odd = state[at : at + 8], state[at + 8 : at + 16]
            rows = slice(8 * slab, 8 * slab + 8)
            mine_ref[pair, h, rows, :] = jnp.where(core == 0, even, odd)
            theirs_ref[pair, h, rows, :] = jnp.where(core == 0, odd, even).astype(BF16)


def whole_state(core, own_ref, got_ref, h):
    slabs = own_ref.shape[2] // 8
    own = [own_ref[pair, h].astype(F32) for pair in range(2)]
    got = [got_ref[pair, h].astype(F32) for pair in range(2)]
    even = [jnp.where(core == 0, own[pair], got[pair]) for pair in range(2)]
    odd = [jnp.where(core == 0, got[pair], own[pair]) for pair in range(2)]
    tiles = []
    for slab in range(slabs):
        for pair in range(2):
            rows = slice(8 * slab, 8 * slab + 8)
            tiles += [even[pair][rows], odd[pair][rows]]
    return jnp.concatenate(tiles, axis=0).astype(BF16)


def cols(h, dim):
    return slice(h * dim, (h + 1) * dim)


def state_kernel(core_ref, k_ref, v_ref, mine_ref, theirs_ref):
    core = core_ref[0]
    dim = mine_ref.shape[3]
    ats = [cols(h, dim) for h in range(mine_ref.shape[1])]
    states = [dot(k_ref[:, at], v_ref[:, at], TN) for at in ats]
    for h, state in enumerate(states):
        put_halves(core, state, h, mine_ref, theirs_ref)


def intra_kernel(q_ref, k_ref, v_ref, scores_ref, intra_ref):
    heads = scores_ref.shape[0]
    dim = q_ref.shape[1] // heads
    causal = causal_mask(q_ref.shape[0])
    ats = [cols(h, dim) for h in range(heads)]
    scores = [
        jnp.where(causal, dot(q_ref[:, at], k_ref[:, at], NT), 0.0).astype(BF16) for at in ats
    ]
    for h, at in enumerate(ats):
        scores_ref[h] = scores[h]
        intra_ref[:, at] = dot(scores[h], v_ref[:, at], NN)


def mix_kernel(core_ref, q_ref, intra_ref, own_ref, got_ref, gain_ref, do_ref, *rest):
    att_ref, gm_ref, prior_ref, mine_ref, theirs_ref = rest[-5:]
    core = core_ref[0]
    heads, dim = own_ref.shape[1], own_ref.shape[3]
    ats = [cols(h, dim) for h in range(heads)]
    for h in range(heads):
        prior_ref[h] = whole_state(core, own_ref, got_ref, h)
    crosses = [dot(q_ref[:, at], prior_ref[h], NN) for h, at in enumerate(ats)]
    for at, cross in zip(ats, crosses):
        mixed = intra_ref[:, at] + cross
        gain = gain_ref[:, at]
        inv = lax.rsqrt(jnp.mean(mixed * mixed, axis=1, keepdims=True) + 1e-06)
        att_ref[:, at] = (gain * mixed * inv).astype(BF16)
        scaled = gain * do_ref[:, at].astype(F32)
        along = jnp.mean(scaled * mixed, axis=1, keepdims=True)
        gm_ref[:, at] = (inv * scaled - mixed * (inv * inv * inv * along)).astype(BF16)
    grads = [dot(q_ref[:, at], gm_ref[:, at], TN) for at in ats]
    for h, grad in enumerate(grads):
        put_halves(core, grad, h, mine_ref, theirs_ref)


def local_grad_kernel(q_ref, k_ref, v_ref, gm_ref, scores_ref, prior_ref, *rest):
    qg_ref, kpart_ref, vpart_ref = rest[-3:]
    heads = scores_ref.shape[0]
    dim = q_ref.shape[1] // heads
    causal = causal_mask(q_ref.shape[0])
    ats = [cols(h, dim) for h in range(heads)]
    grads = [
        jnp.where(causal, dot(gm_ref[:, at], v_ref[:, at], NT), 0.0).astype(BF16) for at in ats
    ]
    for h, at in enumerate(ats):
        qg = dot(grads[h], k_ref[:, at], NN) + dot(gm_ref[:, at], prior_ref[h], NT)
        qg_ref[:, at] = qg.astype(BF16)
    for h, at in enumerate(ats):
        kpart_ref[:, at] = dot(grads[h], q_ref[:, at], TN)
    for h, at in enumerate(ats):
        vpart_ref[:, at] = dot(scores_ref[h], gm_ref[:, at], TN)


def final_kernel(core_ref, k_ref, v_ref, kpart_ref, vpart_ref, own_ref, got_ref, *rest):
    kg_ref, vg_ref = rest[-2:]
    core = core_ref[0]
    heads, dim = own_ref.shape[1], own_ref.shape[3]
    laters = [whole_state(core, own_ref, got_ref, h) for h in range(heads)]
    for h, later in enumerate(laters):
        at = cols(h, dim)
        kg_ref[:, at] = (kpart_ref[:, at] + dot(v_ref[:, at], later, NT)).astype(BF16)
    for h, later in enumerate(laters):
        at = cols(h, dim)
        vg_ref[:, at] = (vpart_ref[:, at] + dot(k_ref[:, at], later, NN)).astype(BF16)


def fused_on_device(n, queries, keys, values, carried_state, gain, out_grad):
    tokens, width = queries.shape
    heads, owned, dim = carried_state.shape
    slab_rows = dim // 4
    bounds = [0]
    for share in CHUNK_EIGHTHS:
        bounds.append(bounds[-1] + heads * share // sum(CHUNK_EIGHTHS))
    chunks = range(len(CHUNK_EIGHTHS))
    rank = lax.axis_index("ctx").astype(jnp.int32)
    core_arg = (rank & 1).reshape(1)
    odd_core, odd_pair = (rank & 1) == 1, (rank & 2) == 2
    odd_slab = {}
    step = 1
    while 4 * step < n:
        odd_slab[step] = (rank & (4 * step)) != 0
        step *= 2
    owned_at = (lax.axis_index("ctx").astype(jnp.uint32) >> 2) * jnp.uint32(owned)
    scalars = (core_arg, odd_core, odd_pair, odd_slab, owned_at)
    scalars, (keys, values, carried_state) = lax.optimization_barrier(
        (scalars, (keys, values, carried_state))
    )
    core_arg, odd_core, odd_pair, odd_slab, owned_at = scalars
    gain_row = gain.reshape(1, width)

    def swap(x, bit):
        return lax.ppermute(x, "ctx", [(i, i ^ bit) for i in range(n)])

    def call(name, body, chunk, ins, outs, flops, with_core=True, keep=(), sub=0, subs=1):
        part = bounds[chunk + 1] - bounds[chunk]
        hb = BLOCKS[name]
        cuts = [part // hb * i // subs for i in range(subs + 1)]
        first, count = cuts[sub], cuts[sub + 1] - cuts[sub]
        off = bounds[chunk] // hb + first
        specs = {
            "flat": pl.BlockSpec((tokens, hb * dim), lambda i, *_: (0, i + off)),
            "row": pl.BlockSpec((1, hb * dim), lambda i, *_: (0, i + off)),
            "half": pl.BlockSpec((2, hb, slab_rows, dim), lambda i, *_: (0, i + first, 0, 0)),
            "sq": pl.BlockSpec((hb, tokens, tokens), lambda i, *_: (i + first, 0, 0)),
            "state": pl.BlockSpec((hb, dim, dim), lambda i, *_: (i + first, 0, 0)),
            "local": pl.BlockSpec((tokens, hb * dim), lambda i, *_: (0, i + first)),
        }
        shapes = {
            "flat": (tokens, width),
            "half": (2, part, slab_rows, dim),
            "sq": (part, tokens, tokens),
            "state": (part, dim, dim),
            "local": (tokens, part * dim),
        }
        scalar_args = [core_arg] if with_core else []
        args = [a for _, a in ins]
        in_specs = [specs[kind] for kind, _ in ins]
        aliases = {}
        for at, array in keep:
            aliases[len(scalar_args) + len(args)] = at
            args.append(array)
            in_specs.append(pl.BlockSpec(memory_space=pl.ANY))
        block = lambda kind: math.prod(specs[kind].block_shape)
        moved = sum(block(kind) * a.dtype.itemsize for kind, a in ins)
        moved += sum(block(kind) * jnp.dtype(t).itemsize for kind, t in outs)
        return pl.pallas_call(
            body,
            out_shape=[jax.ShapeDtypeStruct(shapes[kind], t) for kind, t in outs],
            grid_spec=pltpu.PrefetchScalarGridSpec(
                num_scalar_prefetch=len(scalar_args),
                grid=(count,),
                in_specs=in_specs,
                out_specs=[specs[kind] for kind, _ in outs],
            ),
            input_output_aliases=aliases,
            cost_estimate=pl.CostEstimate(
                flops=flops * count * hb, bytes_accessed=moved * count, transcendentals=0
            ),
            compiler_params=pltpu.CompilerParams(vmem_limit_bytes=VMEM_LIMIT),
        )(*scalar_args, *args)

    def scan_out(mine, theirs, carried=None):
        later = carried is None

        def if_after(odd, x):
            return jnp.where(odd, 0.0, x) if later else jnp.where(odd, x, 0.0)

        def if_before(odd, x):
            return jnp.where(odd, x, 0.0) if later else jnp.where(odd, 0.0, x)

        from_core = swap(theirs, 1).astype(F32)
        chip = mine + from_core
        kept = jnp.where(odd_pair, chip[1], chip[0])
        sent = jnp.where(odd_pair, chip[0], chip[1]).astype(BF16)
        from_pair = swap(sent, 2).astype(F32)
        total = kept + from_pair
        before = 0.0
        last = max(odd_slab)
        for step, odd in odd_slab.items():
            if later:
                got = swap(total.astype(BF16), 4 * step).astype(F32)
                before = before + if_after(odd, got)
                total = total + got
            elif step < last:
                rows = jnp.concatenate([total.astype(BF16), carried], axis=1)
                rows = swap(rows, 4 * step)
                got, other = rows[:, :slab_rows].astype(F32), rows[:, slab_rows:]
                before = before + if_after(odd, got)
                total = total + got
                lower, upper = jnp.where(odd, other, carried), jnp.where(odd, carried, other)
                carried = jnp.concatenate([lower, upper], axis=1)
            else:
                blank = jnp.zeros_like(carried)
                lower, upper = jnp.where(odd, blank, carried), jnp.where(odd, carried, blank)
                known = jnp.concatenate([lower, upper], axis=1).astype(F32)
                sent = (known + if_before(odd, total)).astype(BF16)
                before = before + known + swap(sent, 4 * step).astype(F32)
        for_pair = (before + if_before(odd_pair, kept)).astype(BF16)
        here = before + if_after(odd_pair, from_pair)
        there = swap(for_pair, 2).astype(F32)
        ours = jnp.stack([jnp.where(odd_pair, there, here), jnp.where(odd_pair, here, there)])
        for_core = (ours + if_before(odd_core, mine)).astype(BF16)
        got_half = swap(for_core, 1)
        own_half = (ours + if_after(odd_core, from_core)).astype(BF16)
        return own_half, got_half, total

    mac = 2 * tokens * dim
    states, intras, priors, mixes, locals_ = [], [], [], [], []
    for g in chunks:
        pair = (keys, values)
        if g == 0:
            pair = [pltpu.with_memory_space_constraint(x, pltpu.HBM) for x in pair]
        ins = [("flat", x) for x in pair]
        outs = [("half", F32), ("half", BF16)]
        states.append(call("state", state_kernel, g, ins, outs, mac * dim))
    for g in chunks:
        ins = [("flat", queries), ("flat", keys), ("flat", values)]
        outs = [("sq", BF16), ("local", F32)]
        intras.append(call("intra", intra_kernel, g, ins, outs, 2 * mac * tokens, with_core=False))
    for g in chunks:
        carried = carried_state[bounds[g] : bounds[g + 1]].astype(BF16)
        priors.append(scan_out(*states[g], carried))
    keep = []
    for g in chunks:
        ins = [
            ("flat", queries),
            ("local", intras[g][1]),
            ("half", priors[g][0]),
            ("half", priors[g][1]),
            ("row", gain_row),
            ("flat", out_grad),
        ]
        outs = [("flat", BF16), ("local", BF16), ("state", BF16), ("half", F32), ("half", BF16)]
        mixes.append(call("mix", mix_kernel, g, ins, outs, 2 * mac * dim, keep=keep))
        keep = [(0, mixes[g][0])]
    keep = []
    for g in chunks:
        ins = [
            ("flat", queries),
            ("flat", keys),
            ("flat", values),
            ("local", mixes[g][1]),
            ("sq", intras[g][0]),
            ("state", mixes[g][2]),
        ]
        outs = [("flat", BF16), ("local", F32), ("local", F32)]
        flops = 4 * mac * tokens + mac * dim
        for sub in range(LOCAL_SPLIT):
            at = dict(sub=sub, subs=LOCAL_SPLIT)
            made = call("local", local_grad_kernel, g, ins, outs, flops, False, keep, **at)
            keep = list(enumerate(made))
        locals_.append(made)
        keep = [(0, made[0])]
    laters = [scan_out(mixes[g][3], mixes[g][4]) for g in chunks]
    keep = []
    for g in chunks:
        ins = [
            ("flat", keys),
            ("flat", values),
            ("local", locals_[g][1]),
            ("local", locals_[g][2]),
            ("half", laters[g][0]),
            ("half", laters[g][1]),
        ]
        made = call("final", final_kernel, g, ins, [("flat", BF16)] * 2, 2 * mac * dim, keep=keep)
        keep = list(enumerate(made))
    zero = jnp.uint32(0)
    owned_rows = [
        lax.dynamic_slice(later, (zero, owned_at, zero), later.shape[:1] + (owned, dim))
        for _, _, later in laters
    ]
    state_grad = jnp.concatenate(owned_rows, axis=0)
    return mixes[-1][0], locals_[-1][0], made[0], made[1], state_grad


def on_device(n, queries, keys, values, carried_state, gain, out_grad):
    heads, owned, dim = carried_state.shape
    power = n >= 4 and (n & (n - 1)) == 0
    fits = power and owned % 8 == 0 and owned == 8 and dim % 128 == 0
    if fits and heads % 8 == 0 and queries.shape[0] % 16 == 0:
        return fused_on_device(n, queries, keys, values, carried_state, gain, out_grad)
    return plain_on_device(queries, keys, values, carried_state, gain, out_grad)


def solution(mesh):
    rows = P(("groups", "ctx"), None)
    state = P("groups", "ctx", None)
    return jax.shard_map(
        functools.partial(on_device, mesh.shape["ctx"]),
        mesh=mesh,
        in_specs=(rows, rows, rows, state, P(), rows),
        out_specs=(rows, rows, rows, rows, state),
        check_vma=False,
    )
```

```python
import functools
import math

import jax
import jax.numpy as jnp
from jax import lax
from jax.experimental import pallas as pl
from jax.experimental.pallas import tpu as pltpu
from jax.sharding import PartitionSpec as P


BF16 = jnp.bfloat16
F32 = jnp.float32
CHUNK_EIGHTHS = (4, 4)
BLOCKS = {"state": 8, "intra": 16, "mix": 16, "local": 8, "final": 16}
LOCAL_SPLIT = 2
VMEM_LIMIT = 20 * 1024 * 1024


def causal_mask(count):
    row_ids = lax.broadcasted_iota(jnp.int32, (count, count), 0)
    col_ids = lax.broadcasted_iota(jnp.int32, (count, count), 1)
    return col_ids <= row_ids


def plain_on_device(queries, keys, values, carried_state, gain, out_grad):
    tokens = queries.shape[0]
    heads = carried_state.shape[0]
    head_dim = carried_state.shape[2]
    f32 = dict(preferred_element_type=F32)
    split = lambda a: a.reshape(tokens, heads, head_dim)
    spread = functools.partial(
        lax.all_to_all, axis_name="ctx", split_axis=2, concat_axis=0, tiled=True
    )
    collect = functools.partial(
        lax.all_to_all, axis_name="ctx", split_axis=0, concat_axis=2, tiled=True
    )
    q, k, v = split(queries), split(keys), split(values)
    blocks = spread(jnp.einsum("thd,the->hde", k, v, **f32)[None])
    earlier = jnp.cumsum(blocks, axis=0) - blocks + carried_state[None]
    prior_bf = collect(earlier)[0].astype(BF16)
    causal = causal_mask(tokens)[None]
    scores = jnp.where(causal, jnp.einsum("thd,shd->hts", q, k, **f32), 0.0).astype(BF16)
    mixed = jnp.einsum("hts,she->the", scores, v, **f32)
    mixed = mixed + jnp.einsum("thd,hde->the", q, prior_bf, **f32)
    inv_rms = lax.rsqrt(jnp.mean(mixed * mixed, axis=2, keepdims=True) + 1e-06)
    gain_heads = gain.reshape(1, heads, head_dim)
    attended = (gain_heads * mixed * inv_rms).astype(BF16)
    scaled = gain_heads * split(out_grad).astype(F32)
    grad_mixed = (
        inv_rms * scaled
        - mixed * (inv_rms * inv_rms * inv_rms) * jnp.mean(scaled * mixed, axis=2, keepdims=True)
    ).astype(BF16)
    grads = spread(jnp.einsum("thd,the->hde", q, grad_mixed, **f32)[None])
    inclusive = jnp.cumsum(grads, axis=0)
    total = inclusive[-1:]
    later_bf = collect((total - inclusive).astype(BF16))[0]
    grad_scores = jnp.einsum("the,she->hts", grad_mixed, v, **f32)
    grad_scores = jnp.where(causal, grad_scores, 0.0).astype(BF16)
    q_grad = jnp.einsum("hts,shd->thd", grad_scores, k, **f32)
    q_grad = q_grad + jnp.einsum("the,hde->thd", grad_mixed, prior_bf, **f32)
    k_grad = jnp.einsum("hts,thd->shd", grad_scores, q, **f32)
    k_grad = k_grad + jnp.einsum("she,hde->shd", v, later_bf, **f32)
    v_grad = jnp.einsum("hts,the->she", scores, grad_mixed, **f32)
    v_grad = v_grad + jnp.einsum("shd,hde->she", k, later_bf, **f32)
    flat = lambda a: a.astype(BF16).reshape(tokens, heads * head_dim)
    return flat(attended), flat(q_grad), flat(k_grad), flat(v_grad), total[0]


def dot(a, b, dims):
    return lax.dot_general(a, b, (dims, ((), ())), preferred_element_type=F32)


NN = ((1,), (0,))
NT = ((1,), (1,))
TN = ((0,), (0,))


def put_halves(core, state, h, mine_ref, theirs_ref):
    slabs = mine_ref.shape[2] // 8
    for slab in range(slabs):
        for pair in range(2):
            at = 8 * (4 * slab + 2 * pair)
            even, odd = state[at : at + 8], state[at + 8 : at + 16]
            rows = slice(8 * slab, 8 * slab + 8)
            mine_ref[pair, h, rows, :] = jnp.where(core == 0, even, odd)
            theirs_ref[pair, h, rows, :] = jnp.where(core == 0, odd, even).astype(BF16)


def whole_state(core, own_ref, got_ref, h):
    slabs = own_ref.shape[2] // 8
    own = [own_ref[pair, h].astype(F32) for pair in range(2)]
    got = [got_ref[pair, h].astype(F32) for pair in range(2)]
    even = [jnp.where(core == 0, own[pair], got[pair]) for pair in range(2)]
    odd = [jnp.where(core == 0, got[pair], own[pair]) for pair in range(2)]
    tiles = []
    for slab in range(slabs):
        for pair in range(2):
            rows = slice(8 * slab, 8 * slab + 8)
            tiles += [even[pair][rows], odd[pair][rows]]
    return jnp.concatenate(tiles, axis=0).astype(BF16)


def cols(h, dim):
    return slice(h * dim, (h + 1) * dim)


def state_kernel(core_ref, k_ref, v_ref, mine_ref, theirs_ref):
    core = core_ref[0]
    dim = mine_ref.shape[3]
    ats = [cols(h, dim) for h in range(mine_ref.shape[1])]
    states = [dot(k_ref[:, at], v_ref[:, at], TN) for at in ats]
    for h, state in enumerate(states):
        put_halves(core, state, h, mine_ref, theirs_ref)


def intra_kernel(q_ref, k_ref, v_ref, scores_ref, intra_ref):
    heads = scores_ref.shape[0]
    dim = q_ref.shape[1] // heads
    causal = causal_mask(q_ref.shape[0])
    ats = [cols(h, dim) for h in range(heads)]
    scores = [
        jnp.where(causal, dot(q_ref[:, at], k_ref[:, at], NT), 0.0).astype(BF16) for at in ats
    ]
    for h, at in enumerate(ats):
        scores_ref[h] = scores[h]
        intra_ref[:, at] = dot(scores[h], v_ref[:, at], NN)


def mix_kernel(core_ref, q_ref, intra_ref, own_ref, got_ref, gain_ref, do_ref, *rest):
    att_ref, gm_ref, prior_ref, mine_ref, theirs_ref = rest[-5:]
    core = core_ref[0]
    heads, dim = own_ref.shape[1], own_ref.shape[3]
    ats = [cols(h, dim) for h in range(heads)]
    for h in range(heads):
        prior_ref[h] = whole_state(core, own_ref, got_ref, h)
    crosses = [dot(q_ref[:, at], prior_ref[h], NN) for h, at in enumerate(ats)]
    for at, cross in zip(ats, crosses):
        mixed = intra_ref[:, at] + cross
        gain = gain_ref[:, at] * math.sqrt(dim)
        r = lax.rsqrt(jnp.sum(mixed * mixed, axis=1, keepdims=True) + dim * 1e-06)
        gained = gain * mixed
        att_ref[:, at] = (gained * r).astype(BF16)
        do = do_ref[:, at].astype(F32)
        along = jnp.sum(gained * do, axis=1, keepdims=True)
        gm_ref[:, at] = (r * (gain * do - mixed * (r * r * along))).astype(BF16)
    grads = [dot(q_ref[:, at], gm_ref[:, at], TN) for at in ats]
    for h, grad in enumerate(grads):
        put_halves(core, grad, h, mine_ref, theirs_ref)


def local_grad_kernel(q_ref, k_ref, v_ref, gm_ref, scores_ref, prior_ref, *rest):
    qg_ref, kpart_ref, vpart_ref = rest[-3:]
    heads = scores_ref.shape[0]
    dim = q_ref.shape[1] // heads
    causal = causal_mask(q_ref.shape[0])
    ats = [cols(h, dim) for h in range(heads)]
    grads = [
        jnp.where(causal, dot(gm_ref[:, at], v_ref[:, at], NT), 0.0).astype(BF16) for at in ats
    ]
    for h, at in enumerate(ats):
        qg = dot(grads[h], k_ref[:, at], NN) + dot(gm_ref[:, at], prior_ref[h], NT)
        qg_ref[:, at] = qg.astype(BF16)
    for h, at in enumerate(ats):
        kpart_ref[:, at] = dot(grads[h], q_ref[:, at], TN)
    for h, at in enumerate(ats):
        vpart_ref[:, at] = dot(scores_ref[h], gm_ref[:, at], TN)


def final_kernel(core_ref, k_ref, v_ref, kpart_ref, vpart_ref, own_ref, got_ref, *rest):
    kg_ref, vg_ref = rest[-2:]
    core = core_ref[0]
    heads, dim = own_ref.shape[1], own_ref.shape[3]
    laters = [whole_state(core, own_ref, got_ref, h) for h in range(heads)]
    for h, later in enumerate(laters):
        at = cols(h, dim)
        kg_ref[:, at] = (kpart_ref[:, at] + dot(v_ref[:, at], later, NT)).astype(BF16)
    for h, later in enumerate(laters):
        at = cols(h, dim)
        vg_ref[:, at] = (vpart_ref[:, at] + dot(k_ref[:, at], later, NN)).astype(BF16)


def fused_on_device(n, queries, keys, values, carried_state, gain, out_grad):
    tokens, width = queries.shape
    heads, owned, dim = carried_state.shape
    slab_rows = dim // 4
    bounds = [0]
    for share in CHUNK_EIGHTHS:
        bounds.append(bounds[-1] + heads * share // sum(CHUNK_EIGHTHS))
    chunks = range(len(CHUNK_EIGHTHS))
    rank = lax.axis_index("ctx").astype(jnp.int32)
    core_arg = (rank & 1).reshape(1)
    odd_core, odd_pair = (rank & 1) == 1, (rank & 2) == 2
    odd_slab = {}
    step = 1
    while 4 * step < n:
        odd_slab[step] = (rank & (4 * step)) != 0
        step *= 2
    owned_at = (lax.axis_index("ctx").astype(jnp.uint32) >> 2) * jnp.uint32(owned)
    scalars = (core_arg, odd_core, odd_pair, odd_slab, owned_at)
    scalars, (keys, values, carried_state) = lax.optimization_barrier(
        (scalars, (keys, values, carried_state))
    )
    core_arg, odd_core, odd_pair, odd_slab, owned_at = scalars
    gain_row = gain.reshape(1, width)

    def swap(x, bit):
        return lax.ppermute(x, "ctx", [(i, i ^ bit) for i in range(n)])

    def call(name, body, chunk, ins, outs, flops, with_core=True, keep=(), sub=0, subs=1):
        part = bounds[chunk + 1] - bounds[chunk]
        hb = BLOCKS[name]
        cuts = [part // hb * i // subs for i in range(subs + 1)]
        first, count = cuts[sub], cuts[sub + 1] - cuts[sub]
        off = bounds[chunk] // hb + first
        specs = {
            "flat": pl.BlockSpec((tokens, hb * dim), lambda i, *_: (0, i + off)),
            "row": pl.BlockSpec((1, hb * dim), lambda i, *_: (0, i + off)),
            "half": pl.BlockSpec((2, hb, slab_rows, dim), lambda i, *_: (0, i + first, 0, 0)),
            "sq": pl.BlockSpec((hb, tokens, tokens), lambda i, *_: (i + first, 0, 0)),
            "state": pl.BlockSpec((hb, dim, dim), lambda i, *_: (i + first, 0, 0)),
            "local": pl.BlockSpec((tokens, hb * dim), lambda i, *_: (0, i + first)),
        }
        shapes = {
            "flat": (tokens, width),
            "half": (2, part, slab_rows, dim),
            "sq": (part, tokens, tokens),
            "state": (part, dim, dim),
            "local": (tokens, part * dim),
        }
        scalar_args = [core_arg] if with_core else []
        args = [a for _, a in ins]
        in_specs = [specs[kind] for kind, _ in ins]
        aliases = {}
        for at, array in keep:
            aliases[len(scalar_args) + len(args)] = at
            args.append(array)
            in_specs.append(pl.BlockSpec(memory_space=pl.ANY))
        block = lambda kind: math.prod(specs[kind].block_shape)
        moved = sum(block(kind) * a.dtype.itemsize for kind, a in ins)
        moved += sum(block(kind) * jnp.dtype(t).itemsize for kind, t in outs)
        return pl.pallas_call(
            body,
            out_shape=[jax.ShapeDtypeStruct(shapes[kind], t) for kind, t in outs],
            grid_spec=pltpu.PrefetchScalarGridSpec(
                num_scalar_prefetch=len(scalar_args),
                grid=(count,),
                in_specs=in_specs,
                out_specs=[specs[kind] for kind, _ in outs],
            ),
            input_output_aliases=aliases,
            cost_estimate=pl.CostEstimate(
                flops=flops * count * hb, bytes_accessed=moved * count, transcendentals=0
            ),
            compiler_params=pltpu.CompilerParams(vmem_limit_bytes=VMEM_LIMIT),
        )(*scalar_args, *args)

    def scan_out(mine, theirs, carried=None):
        later = carried is None

        def if_after(odd, x):
            return jnp.where(odd, 0.0, x) if later else jnp.where(odd, x, 0.0)

        def if_before(odd, x):
            return jnp.where(odd, x, 0.0) if later else jnp.where(odd, 0.0, x)

        from_core = swap(theirs, 1).astype(F32)
        chip = mine + from_core
        kept = jnp.where(odd_pair, chip[1], chip[0])
        sent = jnp.where(odd_pair, chip[0], chip[1]).astype(BF16)
        from_pair = swap(sent, 2).astype(F32)
        total = kept + from_pair
        before = 0.0
        last = max(odd_slab)
        for step, odd in odd_slab.items():
            if later:
                got = swap(total.astype(BF16), 4 * step).astype(F32)
                before = before + if_after(odd, got)
                total = total + got
            elif step < last:
                rows = jnp.concatenate([total.astype(BF16), carried], axis=1)
                rows = swap(rows, 4 * step)
                got, other = rows[:, :slab_rows].astype(F32), rows[:, slab_rows:]
                before = before + if_after(odd, got)
                total = total + got
                lower, upper = jnp.where(odd, other, carried), jnp.where(odd, carried, other)
                carried = jnp.concatenate([lower, upper], axis=1)
            else:
                blank = jnp.zeros_like(carried)
                lower, upper = jnp.where(odd, blank, carried), jnp.where(odd, carried, blank)
                known = jnp.concatenate([lower, upper], axis=1).astype(F32)
                sent = (known + if_before(odd, total)).astype(BF16)
                before = before + known + swap(sent, 4 * step).astype(F32)
        for_pair = (before + if_before(odd_pair, kept)).astype(BF16)
        here = before + if_after(odd_pair, from_pair)
        there = swap(for_pair, 2).astype(F32)
        ours = jnp.stack([jnp.where(odd_pair, there, here), jnp.where(odd_pair, here, there)])
        for_core = (ours + if_before(odd_core, mine)).astype(BF16)
        got_half = swap(for_core, 1)
        own_half = (ours + if_after(odd_core, from_core)).astype(BF16)
        return own_half, got_half, total

    mac = 2 * tokens * dim
    states, intras, priors, mixes, locals_ = [], [], [], [], []
    for g in chunks:
        pair = (keys, values)
        if g == 0:
            pair = [pltpu.with_memory_space_constraint(x, pltpu.HBM) for x in pair]
        ins = [("flat", x) for x in pair]
        outs = [("half", F32), ("half", BF16)]
        states.append(call("state", state_kernel, g, ins, outs, mac * dim))
    for g in chunks:
        ins = [("flat", queries), ("flat", keys), ("flat", values)]
        outs = [("sq", BF16), ("local", F32)]
        intras.append(call("intra", intra_kernel, g, ins, outs, 2 * mac * tokens, with_core=False))
    for g in chunks:
        carried = carried_state[bounds[g] : bounds[g + 1]].astype(BF16)
        priors.append(scan_out(*states[g], carried))
    keep = []
    for g in chunks:
        ins = [
            ("flat", queries),
            ("local", intras[g][1]),
            ("half", priors[g][0]),
            ("half", priors[g][1]),
            ("row", gain_row),
            ("flat", out_grad),
        ]
        outs = [("flat", BF16), ("local", BF16), ("state", BF16), ("half", F32), ("half", BF16)]
        mixes.append(call("mix", mix_kernel, g, ins, outs, 2 * mac * dim, keep=keep))
        keep = [(0, mixes[g][0])]
    keep = []
    for g in chunks:
        ins = [
            ("flat", queries),
            ("flat", keys),
            ("flat", values),
            ("local", mixes[g][1]),
            ("sq", intras[g][0]),
            ("state", mixes[g][2]),
        ]
        outs = [("flat", BF16), ("local", F32), ("local", F32)]
        flops = 4 * mac * tokens + mac * dim
        for sub in range(LOCAL_SPLIT):
            at = dict(sub=sub, subs=LOCAL_SPLIT)
            made = call("local", local_grad_kernel, g, ins, outs, flops, False, keep, **at)
            keep = list(enumerate(made))
        locals_.append(made)
        keep = [(0, made[0])]
    laters = [scan_out(mixes[g][3], mixes[g][4]) for g in chunks]
    keep = []
    for g in chunks:
        ins = [
            ("flat", keys),
            ("flat", values),
            ("local", locals_[g][1]),
            ("local", locals_[g][2]),
            ("half", laters[g][0]),
            ("half", laters[g][1]),
        ]
        made = call("final", final_kernel, g, ins, [("flat", BF16)] * 2, 2 * mac * dim, keep=keep)
        keep = list(enumerate(made))
    zero = jnp.uint32(0)
    owned_rows = [
        lax.dynamic_slice(later, (zero, owned_at, zero), later.shape[:1] + (owned, dim))
        for _, _, later in laters
    ]
    state_grad = jnp.concatenate(owned_rows, axis=0)
    return mixes[-1][0], locals_[-1][0], made[0], made[1], state_grad


def on_device(n, queries, keys, values, carried_state, gain, out_grad):
    heads, owned, dim = carried_state.shape
    power = n >= 4 and (n & (n - 1)) == 0
    fits = power and owned % 8 == 0 and owned == 8 and dim % 128 == 0
    even = heads % (len(CHUNK_EIGHTHS) * max(BLOCKS.values())) == 0
    if fits and even and queries.shape[0] % 16 == 0:
        return fused_on_device(n, queries, keys, values, carried_state, gain, out_grad)
    return plain_on_device(queries, keys, values, carried_state, gain, out_grad)


def solution(mesh):
    rows = P(("groups", "ctx"), None)
    state = P("groups", "ctx", None)
    return jax.shard_map(
        functools.partial(on_device, mesh.shape["ctx"]),
        mesh=mesh,
        in_specs=(rows, rows, rows, state, P(), rows),
        out_specs=(rows, rows, rows, rows, state),
        check_vma=False,
    )
```
